32 devices in a mesh: ctx: 16 (over z, y, core), ch: 2 (over x).
Axes of the slice: x: 2, y: 2, z: 4, core: 2. Of those that a mesh axis runs over, the one named last changes fastest.
Arguments:
- projections: bfloat16 [3, 2048, 8192], P(None, 'ctx', 'ch'), may hold values from -150 to 150
- grouped_short_filters: float32 [3, 7, 512], P(None, None, 'ch'), may hold values from -2 to 2
- long_filter: float32 [2048, 8192], P('ctx', 'ch'), may hold values from 0 to 0.5
- norm_gain: float32 [8192], P('ch'), may hold values from 0.1 to 1.9
- out_grad: bfloat16 [2048, 8192], P('ctx', 'ch'), may hold values from -6 to 6
Outputs:
- output: bfloat16 [2048, 8192], P('ctx', 'ch')
- proj_grads: bfloat16 [3, 2048, 8192], P(None, 'ctx', 'ch')
- short_grads: float32 [3, 7, 512], P(None, None, 'ch')
- long_grad: float32 [2048, 8192], P('ctx', 'ch')
- gain_grad: float32 [8192], P('ch')
The draws below stay inside these ranges and needn't reach their ends.
All inputs are finite; a program needn't handle non-finite values.
Results may differ from the reference program's by a relative error of at most 0.0064.
Values may be sent and summed in bfloat16 or wider, within the bound.
No kernel may reach another device: no remote copies, remote signals or barrier semaphores. Data moves between devices by JAX's collectives and lax.ppermute only.
A program may use at most 128 MiB of HBM per device.

```python
import math
import jax
import jax.numpy as jnp
from jax import lax

D = 8192
GROUP = 16
KS = 7
TOTAL_TOKENS = 2048
FILTERS = 512


def draw_projections(key, part):
    key_base = jax.random.fold_in(key, 11)
    key_scale = jax.random.fold_in(key, 12)
    chan_pos = jnp.arange(D, dtype=jnp.float32) / D
    chan_scale = jnp.exp(jax.random.uniform(key_scale, (D,), jnp.float32, 0.0, math.log(10.0)))
    chan_scale = chan_scale * jnp.exp(math.log(3.0) * chan_pos)
    base = jnp.clip(jax.random.normal(key_base, (3, TOTAL_TOKENS, D), jnp.float32), -4.0, 4.0)
    ones_row = jnp.ones((D,), jnp.float32)
    factor = jnp.stack([ones_row, ones_row, chan_scale])[:, None, :]
    return (base * factor).astype(jnp.bfloat16)


def draw_long_filter(key, part):
    key_slow = jax.random.fold_in(key, 21)
    key_fast = jax.random.fold_in(key, 22)
    key_pick = jax.random.fold_in(key, 23)
    key_noise = jax.random.fold_in(key, 24)
    spike_seed_state = jax.random.fold_in(key, 25)
    fast_share = 0.5
    slow_tau = jnp.exp(jax.random.uniform(key_slow, (D,), jnp.float32, math.log(TOTAL_TOKENS), math.log(8.0 * TOTAL_TOKENS)))
    fast_tau = jnp.exp(jax.random.uniform(key_fast, (D,), jnp.float32, math.log(12.0), math.log(20.0)))
    is_fast = jax.random.bernoulli(key_pick, fast_share, (D,))
    decay_len = jnp.where(is_fast, fast_tau, slow_tau)
    amplitude = 1.0 / jnp.sqrt(jnp.minimum(decay_len, float(TOTAL_TOKENS)))
    shift_count = jnp.arange(TOTAL_TOKENS, dtype=jnp.int32)
    decay = jnp.exp(-shift_count.astype(jnp.float32)[:, None] / decay_len[None, :])
    spike_offset_index = jax.random.randint(spike_seed_state, (4,), 1, TOTAL_TOKENS)
    masked_elements = jnp.prod(jnp.where(shift_count[:, None] >= spike_offset_index[None, :], 0.65, 1.0), axis=1)
    noise = jax.random.uniform(key_noise, (TOTAL_TOKENS, D), jnp.float32, 0.5, 1.5)
    return (amplitude[None, :] * decay * masked_elements[:, None] * noise).astype(jnp.float32)


def steps_of(own_key, extent, pieces, low, high):
    def one(position, shards_of):
        steps = jax.random.uniform(jax.random.fold_in(jax.random.fold_in(own_key, 6), position), (shards_of,), jnp.float32, low / len(pieces), high / len(pieces))
        return jnp.repeat(jnp.exp(steps), extent[position] // shards_of).reshape((-1,) + (1,) * (len(extent) - position - 1))

    factor_of = one(*pieces[0])
    for cut in pieces[1:]:
        factor_of = factor_of * one(*cut)
    return factor_of


def normal_values(rng, extent, scale, reach, cuts=(), held_as=jnp.bfloat16):
    entries = scale * jax.random.normal(rng, extent, jnp.float32)
    if cuts:
        entries = entries * steps_of(rng, extent, cuts, -0.22, 0.18)
    return jnp.clip(entries, -reach, reach).astype(held_as)


def setup_inputs(seed: int = 0) -> dict:
    key_list = jax.random.split(jax.random.key(seed), 6)
    projections = draw_projections(jax.random.fold_in(key_list[5], 71), 0)
    grouped_short_filters = normal_values(key_list[1], (3, KS, FILTERS), 0.4, 2.0, ((2, 2),), jnp.float32)
    long_filter = draw_long_filter(jax.random.fold_in(key_list[5], 71), 0)
    norm_gain = jnp.clip(1.0 + 0.18 * jax.random.normal(key_list[3], (D,), jnp.float32), 0.1, 1.9)
    out_grad = normal_values(key_list[4], (TOTAL_TOKENS, D), 1.0, 6.0, ((0, 16), (1, 2)))
    return dict(projections=projections, grouped_short_filters=grouped_short_filters, long_filter=long_filter, norm_gain=norm_gain, out_grad=out_grad)


epsilon = 1e-05
channel_block = 256

def causal_short(signal, filters):
    per_chan = jnp.repeat(filters, GROUP, axis=1)
    padded = jnp.pad(signal, ((KS - 1, 0), (0, 0)))
    length = signal.shape[0]
    conv_sum = jnp.zeros(signal.shape, signal.dtype)
    for tap_idx in range(KS):
        conv_sum = conv_sum + per_chan[tap_idx][None, :] * padded[KS - 1 - tap_idx:KS - 1 - tap_idx + length]
    return (conv_sum, padded)

def block_parts(projections, grouped_short_filters, long_filter, offset):
    length = projections.shape[1]
    period = 2 * length
    features = []
    paddings = []
    for proj_idx in range(3):
        signal = lax.dynamic_slice_in_dim(projections[proj_idx], offset, channel_block, 1).astype(jnp.float32)
        filters = lax.dynamic_slice_in_dim(grouped_short_filters[proj_idx], offset // GROUP, channel_block // GROUP, 1)
        conv_sum, padded = causal_short(signal, filters)
        rounded = lax.optimization_barrier(conv_sum.astype(jnp.bfloat16))
        features.append(rounded.astype(jnp.float32))
        paddings.append(padded)
    filter_cols = lax.dynamic_slice_in_dim(long_filter, offset, channel_block, 1)
    mixed_in = features[1] * features[2]
    spec_u = jnp.fft.rfft(mixed_in, n=period, axis=0)
    spec_h = jnp.fft.rfft(filter_cols, n=period, axis=0)
    conv_out = jnp.fft.irfft(spec_u * spec_h, n=period, axis=0)[:length]
    return (features, paddings, spec_u, spec_h, conv_out)

def reference(projections, grouped_short_filters, long_filter, norm_gain, out_grad):
    length = projections.shape[1]
    width = projections.shape[2]
    period = 2 * length
    starts = jnp.arange(width // channel_block, dtype=jnp.int32) * channel_block

    def forward_block(offset):
        features, paddings, spec_u, spec_h, conv_out = block_parts(projections, grouped_short_filters, long_filter, offset)
        return features[0] * conv_out
    gated_out = lax.map(forward_block, starts)
    gated_out = jnp.transpose(gated_out, (1, 0, 2)).reshape(length, width)
    rscale = lax.rsqrt(lax.optimization_barrier(jnp.mean(gated_out * gated_out, axis=1)) + epsilon)
    normed = gated_out * rscale[:, None]
    output = (normed * norm_gain).astype(jnp.bfloat16)
    gradient_float = out_grad.astype(jnp.float32)
    scaled = gradient_float * norm_gain
    inner_total = lax.optimization_barrier(jnp.mean(scaled * normed, axis=1))
    grad_gated = rscale[:, None] * (scaled - normed * inner_total[:, None])
    gain_grad = lax.optimization_barrier(jnp.sum(gradient_float * normed, axis=0))

    def backward_block(offset):
        features, paddings, spec_u, spec_h, conv_out = block_parts(projections, grouped_short_filters, long_filter, offset)
        grad_cols = lax.dynamic_slice_in_dim(grad_gated, offset, channel_block, 1)
        grad_conv = grad_cols * features[0]
        grad_gate = grad_cols * conv_out
        spec_d = jnp.fft.rfft(grad_conv, n=period, axis=0)
        grad_mix = jnp.fft.irfft(jnp.conj(spec_h) * spec_d, n=period, axis=0)[:length]
        long_cols = jnp.fft.irfft(jnp.conj(spec_u) * spec_d, n=period, axis=0)[:length]
        grad_feats = [grad_gate, grad_mix * features[2], grad_mix * features[1]]
        proj_cols = []
        filter_cols = []
        for proj_idx in range(3):
            filters = lax.dynamic_slice_in_dim(grouped_short_filters[proj_idx], offset // GROUP, channel_block // GROUP, 1)
            per_chan = jnp.repeat(filters, GROUP, axis=1)
            cotangent_widened = jnp.pad(grad_feats[proj_idx], ((0, KS - 1), (0, 0)))
            grad_in = jnp.zeros(grad_feats[proj_idx].shape, grad_feats[proj_idx].dtype)
            tap_terms = []
            for tap_idx in range(KS):
                grad_in = grad_in + per_chan[tap_idx][None, :] * cotangent_widened[tap_idx:tap_idx + length]
                shifted = paddings[proj_idx][KS - 1 - tap_idx:KS - 1 - tap_idx + length]
                tap_prod = lax.optimization_barrier(jnp.sum(grad_feats[proj_idx] * shifted, axis=0))
                tap_terms.append(lax.optimization_barrier(jnp.sum(tap_prod.reshape(channel_block // GROUP, GROUP), axis=1)))
            proj_cols.append(grad_in.astype(jnp.bfloat16))
            filter_cols.append(jnp.stack(tap_terms))
        return (jnp.stack(proj_cols), jnp.stack(filter_cols), long_cols)
    proj_blocks, filter_blocks, long_blocks = lax.map(backward_block, starts)
    proj_grads = jnp.transpose(proj_blocks, (1, 2, 0, 3)).reshape(3, length, width)
    short_grads = jnp.transpose(filter_blocks, (1, 2, 0, 3)).reshape(3, KS, width // GROUP)
    long_grad = jnp.transpose(long_blocks, (1, 0, 2)).reshape(length, width)
    return (output, proj_grads, short_grads, long_grad, gain_grad)
```

```python
import functools
import math

import jax
import jax.numpy as jnp
import numpy as np
from jax import lax
from jax.experimental import pallas as pl
from jax.experimental.pallas import tpu as pltpu
from jax.sharding import PartitionSpec as P

D = 8192
GROUP = 16
KS = 7

epsilon = 1e-05

BLOCK = 256
HALO = 8


def passed_along(block, axis, distance):
    devices = range(lax.axis_size(axis))
    route = [(i - distance, i) for i in devices if i - distance in devices]
    return lax.ppermute(block, axis, route)


def contract(form, left, right):
    return jnp.einsum(form, left, right, precision=lax.Precision.HIGHEST)


def factor_sizes(period):
    inner_len = 1
    while 2 * inner_len * (2 * inner_len) <= period and period % (4 * inner_len) == 0:
        inner_len = inner_len * 2
    return (period // inner_len, inner_len)


def dft_tables(order):
    ordinal_list = jnp.arange(order, dtype=jnp.int32)
    phases = (ordinal_list[:, None] * ordinal_list[None, :] % order).astype(jnp.float32) * (
        2.0 * math.pi / order
    )
    return (jnp.cos(phases), jnp.sin(phases))


def make_tables(outer_len, inner_len):
    period = outer_len * inner_len
    cos_a, sin_a = dft_tables(outer_len)
    cos_b, sin_b = dft_tables(inner_len)
    row_ids = jnp.arange(outer_len, dtype=jnp.int32)[:, None]
    col_ids = jnp.arange(inner_len, dtype=jnp.int32)[None, :]
    phases = (row_ids * col_ids % period).astype(jnp.float32) * (2.0 * math.pi / period)
    return (cos_a, sin_a, cos_b, sin_b, jnp.cos(phases), jnp.sin(phases))


def forward_spectrum(signal, tables):
    cos_a, sin_a, cos_b, sin_b, tw_cos, tw_sin = tables
    outer_len = cos_a.shape[0]
    inner_len = cos_b.shape[0]
    half_len = outer_len // 2
    channels = signal.shape[0]
    grid_rows = signal.reshape(channels, half_len, inner_len)
    real_a = contract("cnb,kn->ckb", grid_rows, cos_a[:, :half_len])
    imag_a = -contract("cnb,kn->ckb", grid_rows, sin_a[:, :half_len])
    real_t = real_a * tw_cos + imag_a * tw_sin
    imag_t = imag_a * tw_cos - real_a * tw_sin
    real_s = contract("ckb,bm->ckm", real_t, cos_b) + contract("ckb,bm->ckm", imag_t, sin_b)
    imag_s = contract("ckb,bm->ckm", imag_t, cos_b) - contract("ckb,bm->ckm", real_t, sin_b)
    return (real_s, imag_s)


def inverse_signal(real_s, imag_s, tables):
    cos_a, sin_a, cos_b, sin_b, tw_cos, tw_sin = tables
    outer_len = cos_a.shape[0]
    inner_len = cos_b.shape[0]
    half_len = outer_len // 2
    channels = real_s.shape[0]
    real_z = contract("ckb,bm->ckm", real_s, cos_b) - contract("ckb,bm->ckm", imag_s, sin_b)
    imag_z = contract("ckb,bm->ckm", imag_s, cos_b) + contract("ckb,bm->ckm", real_s, sin_b)
    real_t = real_z * tw_cos - imag_z * tw_sin
    imag_t = imag_z * tw_cos + real_z * tw_sin
    signal = contract("ckb,kn->cnb", real_t, cos_a[:, :half_len]) - contract(
        "ckb,kn->cnb", imag_t, sin_a[:, :half_len]
    )
    scale_back = 1.0 / (outer_len * inner_len)
    return (signal * scale_back).reshape(channels, half_len * inner_len)


def channel_sum(values):
    return lax.psum(values, "ch")


def narrow_path(projections, grouped_short_filters, long_filter, norm_gain, out_grad):
    tokens = projections.shape[1]
    spread = lax.axis_size("ctx")
    length = tokens * spread
    outer_len, inner_len = factor_sizes(2 * length)
    tables = make_tables(outer_len, inner_len)
    per_chan = jnp.repeat(grouped_short_filters, GROUP, axis=2)
    edge_rows = passed_along(projections[:, tokens - (KS - 1) :, :], "ctx", 1)
    extended = jnp.concatenate([edge_rows, projections], axis=1)
    conv_sum = jnp.zeros(projections.shape, jnp.float32)
    for tap_idx in range(KS):
        window = extended[:, KS - 1 - tap_idx : KS - 1 - tap_idx + tokens, :].astype(jnp.float32)
        conv_sum = conv_sum + per_chan[:, tap_idx, None, :] * window
    features = lax.optimization_barrier(conv_sum.astype(jnp.bfloat16))
    gate_feat = features[0].astype(jnp.float32)
    key_feat = features[1].astype(jnp.float32)
    value_feat = features[2].astype(jnp.float32)
    mixed_in = key_feat * value_feat
    chan_h = lax.all_to_all(long_filter.T, "ctx", split_axis=0, concat_axis=1, tiled=True)
    chan_u = lax.all_to_all(mixed_in.T, "ctx", split_axis=0, concat_axis=1, tiled=True)
    real_u, imag_u = forward_spectrum(chan_u, tables)
    real_h, imaginary_filter = forward_spectrum(chan_h, tables)
    prod_r = real_u * real_h - imag_u * imaginary_filter
    prod_i = real_u * imaginary_filter + imag_u * real_h
    chan_z = inverse_signal(prod_r, prod_i, tables)
    conv_out = lax.all_to_all(chan_z, "ctx", split_axis=1, concat_axis=0, tiled=True).T
    gated_out = gate_feat * conv_out
    sq_total = channel_sum(jnp.sum(gated_out * gated_out, axis=1))
    rscale = lax.rsqrt(sq_total / D + epsilon)
    normed = gated_out * rscale[:, None]
    output = (normed * norm_gain).astype(jnp.bfloat16)
    gradient_float = out_grad.astype(jnp.float32)
    scaled = gradient_float * norm_gain
    inner_total = channel_sum(jnp.sum(scaled * normed, axis=1))
    grad_gated = rscale[:, None] * (scaled - normed * (inner_total / D)[:, None])
    gain_part = jnp.sum(gradient_float * normed, axis=0)
    grad_conv = grad_gated * gate_feat
    grad_gate = grad_gated * conv_out
    cotangent_gate_input = lax.all_to_all(
        grad_conv.T, "ctx", split_axis=0, concat_axis=1, tiled=True
    )
    real_d, imag_d = forward_spectrum(cotangent_gate_input, tables)
    back_r = real_h * real_d + imaginary_filter * imag_d
    back_i = real_h * imag_d - imaginary_filter * real_d
    filt_r = real_u * real_d + imag_u * imag_d
    filt_i = real_u * imag_d - imag_u * real_d
    chan_du = inverse_signal(back_r, back_i, tables)
    chan_dh = inverse_signal(filt_r, filt_i, tables)
    mix_back = lax.all_to_all(chan_du, "ctx", split_axis=1, concat_axis=0, tiled=True)
    filt_back = lax.all_to_all(chan_dh, "ctx", split_axis=1, concat_axis=0, tiled=True)
    grad_mix = mix_back.T
    long_grad = filt_back.T
    grad_feats = jnp.stack([grad_gate, grad_mix * value_feat, grad_mix * key_feat])
    next_rows = passed_along(grad_feats[:, : KS - 1, :], "ctx", -1)
    cotangent_widened = jnp.concatenate([grad_feats, next_rows], axis=1)
    grad_in = jnp.zeros(grad_feats.shape, jnp.float32)
    tap_terms = []
    local_width = projections.shape[2]
    for tap_idx in range(KS):
        grad_in = (
            grad_in
            + per_chan[:, tap_idx, None, :] * cotangent_widened[:, tap_idx : tap_idx + tokens, :]
        )
        window = extended[:, KS - 1 - tap_idx : KS - 1 - tap_idx + tokens, :].astype(jnp.float32)
        tap_prod = jnp.sum(grad_feats * window, axis=1)
        tap_terms.append(jnp.sum(tap_prod.reshape(3, local_width // GROUP, GROUP), axis=2))
    filt_part = jnp.stack(tap_terms, axis=1)
    gain_grad, short_grads = lax.psum((gain_part, filt_part), "ctx")
    return (output, grad_in.astype(jnp.bfloat16), short_grads, long_grad, gain_grad)


F32 = jnp.float32
BF16 = jnp.bfloat16


def two_terms(table):
    high = table.astype(np.float32).astype(jnp.bfloat16)
    low = (table - high.astype(np.float64)).astype(np.float32).astype(jnp.bfloat16)
    return np.asarray(high), np.asarray(low)


def block_tables():
    numbers = np.concatenate([np.arange(0, BLOCK, 2), np.arange(1, BLOCK, 2)])
    turns = (2 * numbers[:, None] + 1) * np.arange(BLOCK)[None, :] % (4 * BLOCK)
    phases = turns.astype(np.float64) * (math.pi / (2 * BLOCK))
    forward = np.concatenate([np.cos(phases), -np.sin(phases)], axis=0)
    return two_terms(forward), two_terms(forward.T / BLOCK)


def mxu(left, right):
    return jnp.dot(left, right, preferred_element_type=F32)


LANES = 128
VMEM = pl.BlockSpec(memory_space=pltpu.VMEM)
ANY = pl.BlockSpec(memory_space=pl.ANY)
MIB = 1024 * 1024


def cost(flops, size):
    return pl.CostEstimate(flops=int(flops), transcendentals=0, bytes_accessed=int(size))


def held(values):
    return pltpu.with_memory_space_constraint(values, pltpu.VMEM)


def streamed(values):
    return pltpu.with_memory_space_constraint(values, pltpu.HBM)


def whole(body, name, args, outs, scratch=(), limit=24, work=0, streams=(), out_streams=(), landed=()):
    size = sum(math.prod(a.shape) * a.dtype.itemsize for a in [*args, *outs])
    return pl.pallas_call(
        body,
        name=name,
        in_specs=[ANY if i in streams else VMEM for i in range(len(args))],
        out_specs=[ANY if i in out_streams else VMEM for i in range(len(outs))],
        out_shape=list(outs),
        scratch_shapes=list(scratch),
        cost_estimate=cost(work, size),
        compiler_params=pltpu.CompilerParams(vmem_limit_bytes=limit * MIB),
    )(*[streamed(a) if i in streams and i not in landed else a for i, a in enumerate(args)])


def kept(shape, dtype):
    return pltpu.VMEM(shape, dtype)


def stored(shape, dtype):
    return pltpu.HBM(shape, dtype)


def each(number, step):
    def body(index, carry):
        step(index)
        return carry

    lax.fori_loop(0, number, body, 0)


def copies(source, target, sems):
    return lambda j: pltpu.make_async_copy(source.at[j], target.at[j], sems.at[j])


def wide_copies(source, target, sems, width):
    lead = (slice(None),) * (len(source.shape) - 1)

    def move(j):
        here = pl.ds(pl.multiple_of(j * width, LANES), width)
        return pltpu.make_async_copy(source.at[(*lead, here)], target.at[j], sems.at[j])

    return move


def wide_stores(source, target, sems, width):
    lead = (slice(None),) * (len(target.shape) - 1)

    def move(j):
        here = pl.ds(pl.multiple_of(j * width, LANES), width)
        return pltpu.make_async_copy(source.at[j], target.at[(*lead, here)], sems.at[j])

    return move


def lane_tile(chunk, width, part=0, size=LANES):
    return pl.ds(pl.multiple_of(chunk * width + part * LANES, LANES), size)


def parts_of(width):
    return [(part, slice(part * LANES, (part + 1) * LANES)) for part in range(width // LANES)]


def to_chunks(values, width):
    tokens, local = values.shape
    count = local // width

    def body(source, target, rows, chunks, in_sems, out_sems):
        arrive = wide_copies(source, rows, in_sems, width)
        leave = copies(chunks, target, out_sems)
        for j in range(count):
            arrive(j).start()
        for j in range(count):
            arrive(j).wait()
            chunks[j] = rows[j].astype(BF16)
            leave(j).start()
        for j in range(count):
            leave(j).wait()

    return whole(
        body,
        "to_chunks",
        [values],
        [stored((count, tokens, width), BF16)],
        [
            pltpu.VMEM((count, tokens, width), F32),
            pltpu.VMEM((count, tokens, width), BF16),
            pltpu.SemaphoreType.DMA((count,)),
            pltpu.SemaphoreType.DMA((count,)),
        ],
        streams=[0],
        out_streams=[0],
        limit=8,
    )[0]


def from_chunks(chunks):
    count, tokens, width = chunks.shape

    def body(source, target, rows, wide, in_sems, out_sems):
        arrive = copies(source, rows, in_sems)

        leave = wide_stores(wide, target, out_sems, width)
        for j in range(count):
            arrive(j).start()
        for j in range(count):
            arrive(j).wait()
            wide[j] = rows[j].astype(F32)
            leave(j).start()
        for j in range(count):
            leave(j).wait()

    return whole(
        body,
        "from_chunks",
        [chunks],
        [stored((tokens, count * width), F32)],
        [
            pltpu.VMEM((count, tokens, width), BF16),
            pltpu.VMEM((count, tokens, width), F32),
            pltpu.SemaphoreType.DMA((count,)),
            pltpu.SemaphoreType.DMA((count,)),
        ],
        landed=[0],
        streams=[0],
        out_streams=[0],
        limit=8,
    )[0]


def three_terms(values):
    first = values.astype(BF16)
    rest = values - first.astype(F32)
    second = rest.astype(BF16)
    third = (rest - second.astype(F32)).astype(BF16)
    return first, second, third


def spread_taps(taps, local, width):
    rows, groups = taps.shape

    def body(t_ref, out_ref):
        terms = three_terms(t_ref[...])

        def step(j):
            group = lax.broadcasted_iota(jnp.int32, (groups, width), 0)
            channel = lax.broadcasted_iota(jnp.int32, (groups, width), 1)
            chosen = group == j * (width // GROUP) + channel // GROUP
            matrix = jnp.where(chosen, 1.0, 0.0).astype(BF16)
            total = mxu(terms[0], matrix) + (mxu(terms[1], matrix) + mxu(terms[2], matrix))
            out_ref[:, lane_tile(j, width, 0, width)] = total

        each(local // width, step)

    work = 4 * rows * groups * local
    return whole(body, "spread_taps", [taps], [shape_of((rows, local), F32)], work=work)[0]


def gather_groups(sums, out_ref, groups, width):
    count, rows, _ = sums.shape
    per_chunk = width // GROUP
    group = lax.broadcasted_iota(jnp.int32, (width, LANES), 1)
    channel = lax.broadcasted_iota(jnp.int32, (width, LANES), 0)
    matrix = jnp.where(group == channel // GROUP, 1.0, 0.0).astype(BF16)
    terms = three_terms(sums[...].reshape(count * rows, width))
    found = mxu(terms[0], matrix) + (mxu(terms[1], matrix) + mxu(terms[2], matrix))
    for tile in range(groups // LANES):
        total = None
        for place in range(LANES // per_chunk):
            j = tile * (LANES // per_chunk) + place
            part = found[j * rows : (j + 1) * rows]
            part = pltpu.roll(part, place * per_chunk, axis=1) if place else part
            total = part if total is None else total + part
        out_ref[:, tile * LANES : (tile + 1) * LANES] = total


def dma(*shape):
    return pltpu.SemaphoreType.DMA(shape)


def short_conv(projections, edges, per_chan, width):
    _, tokens, local = projections.shape
    count = local // width

    def body(p_hbm, e_ref, t_ref, f_hbm, u_hbm, p_ref, feats, chunks, ext, p_sem, f_sem, u_sem):
        arrive = wide_copies(p_hbm, p_ref, p_sem, width)
        keep, leave = wide_stores(feats, f_hbm, f_sem, width), copies(chunks, u_hbm, u_sem)
        each(count, lambda j: arrive(j).start())

        def step(j):
            arrive(j).wait()
            for part, cols in parts_of(width):
                here = lane_tile(j, width, part)
                rows = t_ref[:, here]
                found = []
                for i in range(3):
                    ext[i, :HALO, :] = e_ref[i, :, here].astype(F32)
                    ext[i, HALO:, :] = p_ref[j, i, :, cols].astype(F32)
                    total = None
                    for tap in range(KS):
                        at = i * KS + tap
                        term = rows[at : at + 1] * ext[i, HALO - tap : HALO - tap + tokens, :]
                        total = term if total is None else total + term
                    found.append(total.astype(BF16))
                    feats[j, i, :, cols] = found[i]
                chunks[j, :, cols] = (found[1].astype(F32) * found[2].astype(F32)).astype(BF16)
            keep(j).start()
            leave(j).start()

        def finish(j):
            keep(j).wait()
            leave(j).wait()

        each(count, step)
        each(count, finish)

    return whole(
        body,
        "short_conv",
        [projections, edges, per_chan],
        [stored(projections.shape, BF16), stored((count, tokens, width), BF16)],
        [
            pltpu.VMEM((count, 3, tokens, width), BF16),
            pltpu.VMEM((count, 3, tokens, width), BF16),
            pltpu.VMEM((count, tokens, width), BF16),
            pltpu.VMEM((3, HALO + tokens, LANES), F32),
            dma(count),
            dma(count),
            dma(count),
        ],
        streams=[0],
        out_streams=[0, 1],
        work=42 * tokens * local,
    )


def window_spectrum(blocks, forward):
    count, _, width = blocks.shape
    half = BLOCK // 2

    def body(x_hbm, hi_hbm, lo_hbm, g_hbm, x_ref, hi, lo, g_ref, spec, t_sem, x_sem, g_sem):
        arrive, leave = copies(x_hbm, x_ref, x_sem), copies(g_ref, g_hbm, g_sem)
        moves = [
            pltpu.make_async_copy(hi_hbm, hi, t_sem.at[0]),
            pltpu.make_async_copy(lo_hbm, lo, t_sem.at[1]),
        ]
        for move in moves:
            move.start()
        for b in range(count):
            arrive(b).start()
        for move in moves:
            move.wait()
        for b in range(count):
            now, prev = b % 2, (b + 1) % 2
            arrive(b).wait()
            x = x_ref[b]
            spec[now] = mxu(hi[...], x) + mxu(lo[...], x)
            if b == 0:
                g_ref[0] = spec[0]
            else:
                g_ref[b, :half] = spec[now, :half] - spec[prev, BLOCK : BLOCK + half]
                g_ref[b, half:BLOCK] = spec[now, half:BLOCK] + spec[prev, BLOCK + half :]
                g_ref[b, BLOCK : BLOCK + half] = spec[now, BLOCK : BLOCK + half] + spec[prev, :half]
                g_ref[b, BLOCK + half :] = spec[now, BLOCK + half :] - spec[prev, half:BLOCK]
            leave(b).start()
        for b in range(count):
            leave(b).wait()

    shape = (count, 2 * BLOCK, width)
    return whole(
        body,
        "window_spectrum",
        [blocks, *forward],
        [stored(shape, F32)],
        [
            pltpu.VMEM(blocks.shape, BF16),
            *[pltpu.VMEM(table.shape, BF16) for table in forward],
            pltpu.VMEM(shape, F32),
            pltpu.VMEM((2, 2 * BLOCK, width), F32),
            dma(2),
            dma(count),
            dma(count),
        ],
        landed=[0],
        streams=[0, 1, 2],
        out_streams=[0],
        work=8 * BLOCK * blocks.size,
    )[0]


def block_products(window_ref, spec_ref, out_ref, count, width, adjoint):
    rows = 8

    def step(index):
        r = pl.multiple_of(index * rows, rows)
        for part, cols in parts_of(width):
            real = pl.ds(r, rows)
            imag = pl.ds(pl.multiple_of(r + BLOCK, rows), rows)
            win = [(window_ref[m, real, cols], window_ref[m, imag, cols]) for m in range(count)]
            spec = [(spec_ref[m, real, cols], spec_ref[m, imag, cols]) for m in range(count)]
            for b in range(count):
                acc_r = acc_i = None
                pairs = range(count - b) if adjoint else range(b + 1)
                for m in pairs:
                    wr, wi = win[m]
                    sr, si = spec[b + m] if adjoint else spec[b - m]
                    if adjoint:
                        tr, ti = wr * sr + wi * si, wr * si - wi * sr
                    else:
                        tr, ti = wr * sr - wi * si, wr * si + wi * sr
                    acc_r = tr if acc_r is None else acc_r + tr
                    acc_i = ti if acc_i is None else acc_i + ti
                out_ref[b, real, cols] = acc_r
                out_ref[b, imag, cols] = acc_i

    each(BLOCK // rows, step)


def inverse_block(prod, hi, lo):
    top = prod.astype(BF16)
    rest = (prod - top.astype(F32)).astype(BF16)
    return mxu(hi, top) + (mxu(lo, top) + mxu(hi, rest))


def convolve(blocks, window, tables, adjoint):
    count, _, width = blocks.shape
    args = [blocks, window, *sum(tables, ())]

    def body(*refs):
        sources, refs = refs[:6], refs[6:]
        y_hbm, s_hbm, refs = (refs[0], refs[1], refs[2:]) if adjoint else (refs[0], None, refs[1:])
        x_ref, w_ref, fh, fl, th, tl, spec, prod, y_ref, t_sem, x_sem, y_sem, s_sem = refs
        arrive, leave = copies(sources[0], x_ref, x_sem), copies(y_ref, y_hbm, y_sem)
        loads = [
            pltpu.make_async_copy(sources[n], target, t_sem.at[n])
            for n, target in [(2, fh), (3, fl), (1, w_ref), (4, th), (5, tl)]
        ]
        loads[0].start()
        loads[1].start()
        for b in range(count):
            arrive(b).start()
        for move in loads[2:]:
            move.start()
        loads[0].wait()
        loads[1].wait()
        for b in range(count):
            arrive(b).wait()
            x = x_ref[b]
            spec[b] = mxu(fh[...], x) + mxu(fl[...], x)
            if adjoint:
                copies(spec, s_hbm, s_sem)(b).start()
        for move in loads[2:]:
            move.wait()
        block_products(w_ref, spec, prod, count, width, adjoint)
        for b in range(count):
            y_ref[b] = inverse_block(prod[b], th[...], tl[...]).astype(BF16)
            leave(b).start()
        for b in range(count):
            leave(b).wait()
            if adjoint:
                copies(spec, s_hbm, s_sem)(b).wait()

    outs = [stored(blocks.shape, BF16)]
    if adjoint:
        outs.append(stored(window.shape, F32))
    return whole(
        body,
        "correlate_blocks" if adjoint else "convolve",
        args,
        outs,
        [
            *[pltpu.VMEM(a.shape, a.dtype) for a in args],
            pltpu.VMEM(window.shape, F32),
            pltpu.VMEM(window.shape, F32),
            pltpu.VMEM(blocks.shape, BF16),
            dma(6),
            dma(count),
            dma(count),
            dma(count),
        ],
        landed=[0],
        streams=range(6),
        out_streams=range(len(outs)),
        work=20 * BLOCK * blocks.size,
    )


def correlate(spectrum, window, inverse):
    count, _, width = spectrum.shape
    shape = (count, BLOCK, width)
    args = [spectrum, window, *inverse]

    def body(*refs):
        sources, y_hbm, targets = refs[:4], refs[4], refs[5:9]
        prod, y_ref, t_sem, y_sem = refs[9:]
        leave = copies(y_ref, y_hbm, y_sem)
        loads = [pltpu.make_async_copy(sources[n], targets[n], t_sem.at[n]) for n in range(4)]
        for move in loads:
            move.start()
        for move in loads:
            move.wait()
        s_ref, w_ref, th, tl = targets
        block_products(w_ref, s_ref, prod, count, width, True)
        for b in range(count):
            y_ref[b] = inverse_block(prod[b], th[...], tl[...]).astype(BF16)
            leave(b).start()
        for b in range(count):
            leave(b).wait()

    return whole(
        body,
        "correlate",
        args,
        [stored(shape, BF16)],
        [
            *[pltpu.VMEM(a.shape, a.dtype) for a in args],
            pltpu.VMEM(window.shape, F32),
            pltpu.VMEM(shape, BF16),
            dma(4),
            dma(count),
        ],
        streams=range(4),
        out_streams=[0],
        work=12 * BLOCK * spectrum.size,
    )[0]


def row_sums(features, conv, gain, out_grad):
    count, tokens, width = conv.shape

    def body(q_hbm, c_hbm, g_ref, o_hbm, s_ref, q_ref, z_ref, o_ref, acc, q_sem, z_sem, o_sem):
        moves = [
            copies(c_hbm, z_ref, z_sem),
            wide_copies(q_hbm.at[0], q_ref, q_sem, width),
            wide_copies(o_hbm, o_ref, o_sem, width),
        ]

        def begin(j):
            for move in moves:
                move(j).start()

        each(count, begin)
        acc[...] = jnp.zeros_like(acc)

        def step(j):
            for move in moves:
                move(j).wait()
            for part, cols in parts_of(width):
                gated = q_ref[j, :, cols].astype(F32) * z_ref[j, :, cols].astype(F32)
                scaled = o_ref[j, :, cols].astype(F32) * g_ref[:, lane_tile(j, width, part)]
                acc[0] += gated * gated
                acc[1] += scaled * gated

        each(count, step)
        lane = lax.broadcasted_iota(jnp.int32, (tokens, LANES), 1)
        first = jnp.sum(acc[0], axis=1, keepdims=True)
        second = jnp.sum(acc[1], axis=1, keepdims=True)
        s_ref[...] = jnp.where(lane == 0, first, second).T[:8, :]

    return whole(
        body,
        "row_sums",
        [features, conv, gain, out_grad],
        [kept((8, tokens), F32), *[kept(conv.shape, BF16)] * 3],
        [pltpu.VMEM((2, tokens, LANES), F32), dma(count), dma(count), dma(count)],
        landed=[1],
        streams=[0, 1, 3],
        work=6 * conv.size,
    )


def row_scales(sums, tokens):
    turned = jnp.concatenate([sums] * (tokens // 8), axis=0).T
    rscale = lax.rsqrt(turned[:, 0:1] * (1.0 / D) + epsilon)
    return rscale, rscale * turned[:, 1:2] * (1.0 / D)


def conv_grads(gate, conv, out_grad, gain, own_sums, other_sums):
    count, tokens, width = conv.shape

    def body(q_ref, z_ref, o_ref, g_ref, s_ref, r_ref, d_hbm, t_hbm, chunks, total, d_sem, t_sem):
        leave = copies(chunks, d_hbm, d_sem)
        total[...] = s_ref[...] + r_ref[...]
        keep = pltpu.make_async_copy(total, t_hbm, t_sem.at[0])
        keep.start()
        rscale, inner = row_scales(total[...], tokens)
        factor = rscale * inner * rscale
        rscale = jnp.broadcast_to(rscale, (tokens, LANES))
        factor = jnp.broadcast_to(factor, (tokens, LANES))

        def step(j):
            for part, cols in parts_of(width):
                gate_feat = q_ref[j, :, cols].astype(F32)
                gated = gate_feat * z_ref[j, :, cols].astype(F32)
                scaled = o_ref[j, :, cols].astype(F32) * g_ref[:, lane_tile(j, width, part)]
                grad = (rscale * scaled - factor * gated) * gate_feat
                chunks[j, :, cols] = grad.astype(BF16)
            leave(j).start()

        each(count, step)
        keep.wait()
        each(count, lambda j: leave(j).wait())

    return whole(
        body,
        "conv_grads",
        [*map(held, [gate, conv, out_grad]), gain, held(own_sums), other_sums],
        [stored(conv.shape, BF16), stored(own_sums.shape, F32)],
        [pltpu.VMEM(conv.shape, BF16), pltpu.VMEM(own_sums.shape, F32), dma(count), dma(1)],
        out_streams=[0, 1],
        work=8 * conv.size,
    )


def norm_outputs(features, conv, gain, out_grad, sums, projections, edges, groups):
    count, tokens, width = conv.shape
    local = count * width

    def body(q_hbm, c_hbm, g_ref, o_hbm, s_ref, p_hbm, e_ref, out_hbm, gg_hbm, rows_ref, *scratch):
        q_ref, z_ref, o_ref, p_ref, out, gg, ext, sums, gains, sems, out_sem, gg_sem = scratch
        moves = [
            copies(c_hbm, z_ref, sems.at[0]),
            wide_copies(q_hbm.at[0], q_ref, sems.at[1], width),
            wide_copies(o_hbm, o_ref, sems.at[2], width),
            wide_copies(p_hbm.at[0], p_ref, sems.at[3], width),
        ]
        stores = [wide_stores(out, out_hbm, out_sem, width), wide_stores(gg, gg_hbm, gg_sem, width)]

        def begin(j):
            for move in moves:
                move(j).start()

        each(count, begin)
        sums[...] = jnp.zeros_like(sums)
        rscale, inner = row_scales(s_ref[...], tokens)
        rscale = jnp.broadcast_to(rscale, (tokens, LANES))
        inner = jnp.broadcast_to(inner, (tokens, LANES))

        def step(j):
            for move in moves:
                move(j).wait()
            for part, cols in parts_of(width):
                here = lane_tile(j, width, part)
                conv_out = z_ref[j, :, cols].astype(F32)
                grad = o_ref[j, :, cols].astype(F32)
                gain_row = g_ref[:, here]
                normed = q_ref[j, :, cols].astype(F32) * conv_out * rscale
                out[j, :, cols] = (normed * gain_row).astype(BF16)
                grad_gated = rscale * (grad * gain_row - normed * inner)
                own = grad_gated * conv_out
                gg[j, :, cols] = own.astype(BF16)
                gains[:, here] = jnp.sum(grad * normed, axis=0, keepdims=True)
                before, values = e_ref[0, :, here], p_ref[j, :, cols]
                tap_sums(own, before, values, ext, sums, j, 0, cols, tokens)
            for store in stores:
                store(j).start()

        def finish(j):
            for store in stores:
                store(j).wait()

        each(count, step)
        for j in range(count):
            rows_ref[j : j + 1] = gains[:, j * width : (j + 1) * width]
        gather_groups(sums, rows_ref.at[count:], groups, width)
        each(count, finish)

    chunk = pltpu.VMEM(conv.shape, BF16)
    return whole(
        body,
        "norm_outputs",
        [features, conv, gain, out_grad, sums, projections, edges],
        [
            stored((tokens, local), BF16),
            stored((tokens, local), BF16),
            shape_of((count + KS + 1, groups), F32),
        ],
        [
            *[chunk] * 6,
            pltpu.VMEM((HALO + tokens, LANES), F32),
            pltpu.VMEM((count, KS + 1, width), F32),
            pltpu.VMEM((1, local), F32),
            dma(4, count),
            dma(count),
            dma(count),
        ],
        landed=[1],
        streams=[0, 1, 3, 5],
        out_streams=[0, 1],
        work=28 * conv.size,
    )


def shape_of(shape, dtype):
    return jax.ShapeDtypeStruct(shape, dtype)


def tap_sums(own, before, values, ext, sums, j, first, cols, tokens):
    ext[:HALO, :] = before.astype(F32)
    ext[HALO:, :] = values.astype(F32)
    for tap in range(KS):
        total = jnp.sum(own * ext[HALO - tap : HALO - tap + tokens, :], axis=0, keepdims=True)
        sums[j, first + tap : first + tap + 1, cols] = total


def mix_tap_sums(mix, features, projections, edges, groups):
    count, tokens, width = mix.shape
    local = count * width

    def body(m_hbm, f_hbm, p_hbm, e_ref, out_ref, m_ref, f_ref, p_ref, ext, sums, sems):
        moves = [
            copies(m_hbm, m_ref, sems.at[0]),
            wide_copies(f_hbm.at[1:], f_ref, sems.at[1], width),
            wide_copies(p_hbm.at[1:], p_ref, sems.at[2], width),
        ]

        def begin(j):
            for move in moves:
                move(j).start()

        each(count, begin)
        sums[...] = jnp.zeros_like(sums)

        def step(j):
            for move in moves:
                move(j).wait()
            for part, cols in parts_of(width):
                here = lane_tile(j, width, part)
                mixed = m_ref[j, :, cols].astype(F32)
                for i in (1, 2):
                    own = mixed * f_ref[j, 2 - i, :, cols].astype(F32)
                    before, values = e_ref[i, :, here], p_ref[j, i - 1, :, cols]
                    tap_sums(own, before, values, ext, sums, j, (i - 1) * KS, cols, tokens)

        each(count, step)
        gather_groups(sums, out_ref, groups, width)

    return whole(
        body,
        "mix_tap_sums",
        [mix, features, projections, edges],
        [shape_of((2 * KS + 2, groups), F32)],
        [
            pltpu.VMEM(mix.shape, BF16),
            pltpu.VMEM((count, 2, tokens, width), BF16),
            pltpu.VMEM((count, 2, tokens, width), BF16),
            pltpu.VMEM((HALO + tokens, LANES), F32),
            pltpu.VMEM((count, 2 * KS + 2, width), F32),
            dma(3, count),
        ],
        landed=[0],
        streams=[0, 1, 2],
        work=28 * tokens * local,
    )[0]


def proj_grads_of(mix, mix_halo, gate_grad, gate_halo, features, feat_halo, per_chan):
    count, tokens, width = mix.shape
    local = count * width

    def body(m_hbm, mh_ref, gg_hbm, gh_ref, f_hbm, fh_ref, t_ref, o_hbm, *scratch):
        m_ref, gg_ref, f_ref, out, grads, sems, out_sem = scratch
        moves = [
            copies(m_hbm, m_ref, sems.at[0]),
            wide_copies(gg_hbm, gg_ref, sems.at[1], width),
            wide_copies(f_hbm.at[1:], f_ref, sems.at[2], width),
        ]
        leave = wide_stores(out, o_hbm, out_sem, width)

        def begin(j):
            for move in moves:
                move(j).start()

        each(count, begin)

        def step(j):
            for move in moves:
                move(j).wait()
            for part, cols in parts_of(width):
                here = lane_tile(j, width, part)
                rows = t_ref[:, here]
                mixed = m_ref[j, :, cols].astype(F32)
                mixed_after = mh_ref[j, :, cols].astype(F32)
                for i in range(3):
                    if i == 0:
                        own = gg_ref[j, :, cols].astype(F32)
                        after = gh_ref[:, here].astype(F32)
                    else:
                        own = mixed * f_ref[j, 2 - i, :, cols].astype(F32)
                        after = mixed_after * fh_ref[3 - i, :, here].astype(F32)
                    grads[i, :tokens, :] = own
                    grads[i, tokens:, :] = after
                    total = None
                    for tap in range(KS):
                        at = i * KS + tap
                        term = rows[at : at + 1] * grads[i, tap : tap + tokens, :]
                        total = term if total is None else total + term
                    out[j, i, :, cols] = total.astype(BF16)
            leave(j).start()

        each(count, step)
        each(count, lambda j: leave(j).wait())

    return whole(
        body,
        "proj_grads",
        [mix, mix_halo, gate_grad, gate_halo, features, feat_halo, per_chan],
        [stored((3, tokens, local), BF16)],
        [
            pltpu.VMEM(mix.shape, BF16),
            pltpu.VMEM(mix.shape, BF16),
            pltpu.VMEM((count, 2, tokens, width), BF16),
            pltpu.VMEM((count, 3, tokens, width), BF16),
            pltpu.VMEM((3, HALO + tokens, LANES), F32),
            dma(3, count),
            dma(count),
        ],
        landed=[0],
        streams=[0, 2, 4],
        out_streams=[0],
        work=48 * tokens * local,
    )[0]


def exchange(values, axis, distance):
    size = lax.axis_size(axis)
    return lax.ppermute(values, axis, [(i, i ^ distance) for i in range(size)])


def butterfly_sum(values, axis):
    distance = 1
    while distance < lax.axis_size(axis):
        values = values + exchange(values, axis, distance)
        distance *= 2
    return values


def swap_blocks(chunks):
    return lax.all_to_all(chunks, "ctx", split_axis=0, concat_axis=0, tiled=True)


def together(*values):
    return lax.optimization_barrier(values)


def kernel_path(projections, grouped_short_filters, long_filter, norm_gain, out_grad):
    tokens, local = projections.shape[1:]
    spread = lax.axis_size("ctx")
    width = local // spread
    count = tokens * spread // BLOCK
    groups = local // GROUP

    def as_blocks(chunks):
        return chunks.reshape(count, BLOCK, width)

    def as_chunks(blocks):
        return blocks.reshape(spread, tokens, width)

    taps = jnp.pad(grouped_short_filters.reshape(3 * KS, groups), ((0, 3), (0, 0)))
    edges = passed_along(projections[:, tokens - HALO :, :], "ctx", 1)
    sent_h = to_chunks(long_filter, width)
    edges, sent_h = together(edges, sent_h)
    chan_h = swap_blocks(sent_h)
    tables = forward, inverse = jax.tree.map(jnp.asarray, block_tables())
    gain = norm_gain.reshape(1, local)
    per_chan = spread_taps(taps, local, width)
    features, mixed = short_conv(projections, edges, per_chan, width)
    chan_h, mixed = together(chan_h, mixed)
    chan_u = swap_blocks(mixed)
    window_h = window_spectrum(as_blocks(chan_h), forward)
    feat_halo = passed_along(features[:, :HALO, :], "ctx", -1)
    chan_u, window_h, feat_halo = together(chan_u, window_h, feat_halo)
    (chan_z,) = convolve(as_blocks(chan_u), window_h, tables, False)
    conv = swap_blocks(as_chunks(chan_z))
    window_u = window_spectrum(as_blocks(chan_u), forward)
    conv, window_u = together(conv, window_u)
    own_sums, *near = row_sums(features, conv, gain, out_grad)
    grad_conv, sums = conv_grads(*near, gain, own_sums, exchange(own_sums, "ch", 1))
    chan_d = swap_blocks(grad_conv)
    output, gate_grad, early = norm_outputs(
        features, conv, gain, out_grad, sums, projections, edges, groups
    )
    gate_halo = passed_along(gate_grad[:HALO, :], "ctx", -1)
    chan_d, output, gate_grad, early = together(chan_d, output, gate_grad, early)
    chan_du, spec_d = convolve(as_blocks(chan_d), window_h, tables, True)
    mix = swap_blocks(as_chunks(chan_du))
    chan_dh = correlate(spec_d, window_u, inverse)
    chan_dh, early = together(chan_dh, early)
    early = butterfly_sum(early, "ctx")
    mix, chan_dh, gate_halo, early = together(mix, chan_dh, gate_halo, early)
    filt = swap_blocks(as_chunks(chan_dh))
    mix_halo = passed_along(mix[:, :HALO, :], "ctx", -1)
    late = mix_tap_sums(mix, features, projections, edges, groups)
    late = butterfly_sum(late, "ctx")
    proj_grads = proj_grads_of(mix, mix_halo, gate_grad, gate_halo, features, feat_halo, per_chan)
    short_grads = jnp.concatenate([early[spread : spread + KS], late[: 2 * KS]], axis=0)
    return (
        output,
        proj_grads,
        short_grads.reshape(3, KS, groups),
        from_chunks(filt),
        early[:spread].reshape(local),
    )


def on_device(projections, grouped_short_filters, long_filter, norm_gain, out_grad):
    tokens, local = projections.shape[1:]
    spread = lax.axis_size("ctx")
    width = local // spread
    length = tokens * spread
    whole_tiles = width % LANES == 0 and tokens == LANES and length % BLOCK == 0
    pairs = spread & (spread - 1) == 0 and lax.axis_size("ch") == 2
    fits = whole_tiles and pairs and length <= 8 * BLOCK and width == local // GROUP
    path = kernel_path if fits else narrow_path
    return path(projections, grouped_short_filters, long_filter, norm_gain, out_grad)


def solution(mesh):
    in_specs = (P(None, "ctx", "ch"), P(None, None, "ch"), P("ctx", "ch"), P("ch"), P("ctx", "ch"))
    out_specs = (P("ctx", "ch"), P(None, "ctx", "ch"), P(None, None, "ch"), P("ctx", "ch"), P("ch"))
    return jax.shard_map(
        on_device, mesh=mesh, in_specs=in_specs, out_specs=out_specs, check_vma=False
    )
```

```python
import math

import jax
import jax.numpy as jnp
import numpy as np
from jax import lax
from jax.experimental import pallas as pl
from jax.experimental.pallas import tpu as pltpu
from jax.sharding import PartitionSpec as P


D = 8192
GROUP = 16
KS = 7

epsilon = 1e-05

BLOCK = 256
HALO = 8


def passed_along(block, axis, distance):
    devices = range(lax.axis_size(axis))
    route = [(i - distance, i) for i in devices if i - distance in devices]
    return lax.ppermute(block, axis, route)


def contract(form, left, right):
    return jnp.einsum(form, left, right, precision=lax.Precision.HIGHEST)


def factor_sizes(period):
    inner_len = 1
    while 2 * inner_len * (2 * inner_len) <= period and period % (4 * inner_len) == 0:
        inner_len = inner_len * 2
    return (period // inner_len, inner_len)


def dft_tables(order):
    ordinal_list = jnp.arange(order, dtype=jnp.int32)
    phases = (ordinal_list[:, None] * ordinal_list[None, :] % order).astype(jnp.float32) * (
        2.0 * math.pi / order
    )
    return (jnp.cos(phases), jnp.sin(phases))


def make_tables(outer_len, inner_len):
    period = outer_len * inner_len
    cos_a, sin_a = dft_tables(outer_len)
    cos_b, sin_b = dft_tables(inner_len)
    row_ids = jnp.arange(outer_len, dtype=jnp.int32)[:, None]
    col_ids = jnp.arange(inner_len, dtype=jnp.int32)[None, :]
    phases = (row_ids * col_ids % period).astype(jnp.float32) * (2.0 * math.pi / period)
    return (cos_a, sin_a, cos_b, sin_b, jnp.cos(phases), jnp.sin(phases))


def forward_spectrum(signal, tables):
    cos_a, sin_a, cos_b, sin_b, tw_cos, tw_sin = tables
    outer_len = cos_a.shape[0]
    inner_len = cos_b.shape[0]
    half_len = outer_len // 2
    channels = signal.shape[0]
    grid_rows = signal.reshape(channels, half_len, inner_len)
    real_a = contract("cnb,kn->ckb", grid_rows, cos_a[:, :half_len])
    imag_a = -contract("cnb,kn->ckb", grid_rows, sin_a[:, :half_len])
    real_t = real_a * tw_cos + imag_a * tw_sin
    imag_t = imag_a * tw_cos - real_a * tw_sin
    real_s = contract("ckb,bm->ckm", real_t, cos_b) + contract("ckb,bm->ckm", imag_t, sin_b)
    imag_s = contract("ckb,bm->ckm", imag_t, cos_b) - contract("ckb,bm->ckm", real_t, sin_b)
    return (real_s, imag_s)


def inverse_signal(real_s, imag_s, tables):
    cos_a, sin_a, cos_b, sin_b, tw_cos, tw_sin = tables
    outer_len = cos_a.shape[0]
    inner_len = cos_b.shape[0]
    half_len = outer_len // 2
    channels = real_s.shape[0]
    real_z = contract("ckb,bm->ckm", real_s, cos_b) - contract("ckb,bm->ckm", imag_s, sin_b)
    imag_z = contract("ckb,bm->ckm", imag_s, cos_b) + contract("ckb,bm->ckm", real_s, sin_b)
    real_t = real_z * tw_cos - imag_z * tw_sin
    imag_t = imag_z * tw_cos + real_z * tw_sin
    signal = contract("ckb,kn->cnb", real_t, cos_a[:, :half_len]) - contract(
        "ckb,kn->cnb", imag_t, sin_a[:, :half_len]
    )
    scale_back = 1.0 / (outer_len * inner_len)
    return (signal * scale_back).reshape(channels, half_len * inner_len)


def channel_sum(values):
    return lax.psum(values, "ch")


def narrow_path(projections, grouped_short_filters, long_filter, norm_gain, out_grad):
    tokens = projections.shape[1]
    spread = lax.axis_size("ctx")
    length = tokens * spread
    outer_len, inner_len = factor_sizes(2 * length)
    tables = make_tables(outer_len, inner_len)
    per_chan = jnp.repeat(grouped_short_filters, GROUP, axis=2)
    edge_rows = passed_along(projections[:, tokens - (KS - 1) :, :], "ctx", 1)
    extended = jnp.concatenate([edge_rows, projections], axis=1)
    conv_sum = jnp.zeros(projections.shape, jnp.float32)
    for tap_idx in range(KS):
        window = extended[:, KS - 1 - tap_idx : KS - 1 - tap_idx + tokens, :].astype(jnp.float32)
        conv_sum = conv_sum + per_chan[:, tap_idx, None, :] * window
    features = lax.optimization_barrier(conv_sum.astype(jnp.bfloat16))
    gate_feat = features[0].astype(jnp.float32)
    key_feat = features[1].astype(jnp.float32)
    value_feat = features[2].astype(jnp.float32)
    mixed_in = key_feat * value_feat
    chan_h = lax.all_to_all(long_filter.T, "ctx", split_axis=0, concat_axis=1, tiled=True)
    chan_u = lax.all_to_all(mixed_in.T, "ctx", split_axis=0, concat_axis=1, tiled=True)
    real_u, imag_u = forward_spectrum(chan_u, tables)
    real_h, imaginary_filter = forward_spectrum(chan_h, tables)
    prod_r = real_u * real_h - imag_u * imaginary_filter
    prod_i = real_u * imaginary_filter + imag_u * real_h
    chan_z = inverse_signal(prod_r, prod_i, tables)
    conv_out = lax.all_to_all(chan_z, "ctx", split_axis=1, concat_axis=0, tiled=True).T
    gated_out = gate_feat * conv_out
    sq_total = channel_sum(jnp.sum(gated_out * gated_out, axis=1))
    rscale = lax.rsqrt(sq_total / D + epsilon)
    normed = gated_out * rscale[:, None]
    output = (normed * norm_gain).astype(jnp.bfloat16)
    gradient_float = out_grad.astype(jnp.float32)
    scaled = gradient_float * norm_gain
    inner_total = channel_sum(jnp.sum(scaled * normed, axis=1))
    grad_gated = rscale[:, None] * (scaled - normed * (inner_total / D)[:, None])
    gain_part = jnp.sum(gradient_float * normed, axis=0)
    grad_conv = grad_gated * gate_feat
    grad_gate = grad_gated * conv_out
    cotangent_gate_input = lax.all_to_all(
        grad_conv.T, "ctx", split_axis=0, concat_axis=1, tiled=True
    )
    real_d, imag_d = forward_spectrum(cotangent_gate_input, tables)
    back_r = real_h * real_d + imaginary_filter * imag_d
    back_i = real_h * imag_d - imaginary_filter * real_d
    filt_r = real_u * real_d + imag_u * imag_d
    filt_i = real_u * imag_d - imag_u * real_d
    chan_du = inverse_signal(back_r, back_i, tables)
    chan_dh = inverse_signal(filt_r, filt_i, tables)
    mix_back = lax.all_to_all(chan_du, "ctx", split_axis=1, concat_axis=0, tiled=True)
    filt_back = lax.all_to_all(chan_dh, "ctx", split_axis=1, concat_axis=0, tiled=True)
    grad_mix = mix_back.T
    long_grad = filt_back.T
    grad_feats = jnp.stack([grad_gate, grad_mix * value_feat, grad_mix * key_feat])
    next_rows = passed_along(grad_feats[:, : KS - 1, :], "ctx", -1)
    cotangent_widened = jnp.concatenate([grad_feats, next_rows], axis=1)
    grad_in = jnp.zeros(grad_feats.shape, jnp.float32)
    tap_terms = []
    local_width = projections.shape[2]
    for tap_idx in range(KS):
        grad_in = (
            grad_in
            + per_chan[:, tap_idx, None, :] * cotangent_widened[:, tap_idx : tap_idx + tokens, :]
        )
        window = extended[:, KS - 1 - tap_idx : KS - 1 - tap_idx + tokens, :].astype(jnp.float32)
        tap_prod = jnp.sum(grad_feats * window, axis=1)
        tap_terms.append(jnp.sum(tap_prod.reshape(3, local_width // GROUP, GROUP), axis=2))
    filt_part = jnp.stack(tap_terms, axis=1)
    gain_grad, short_grads = lax.psum((gain_part, filt_part), "ctx")
    return (output, grad_in.astype(jnp.bfloat16), short_grads, long_grad, gain_grad)


F32 = jnp.float32
BF16 = jnp.bfloat16


def two_terms(table):
    high = table.astype(np.float32).astype(jnp.bfloat16)
    low = (table - high.astype(np.float64)).astype(np.float32).astype(jnp.bfloat16)
    return np.asarray(high), np.asarray(low)


def block_tables():
    numbers = np.concatenate([np.arange(0, BLOCK, 2), np.arange(1, BLOCK, 2)])
    turns = (2 * numbers[:, None] + 1) * np.arange(BLOCK)[None, :] % (4 * BLOCK)
    phases = turns.astype(np.float64) * (math.pi / (2 * BLOCK))
    forward = np.concatenate([np.cos(phases), -np.sin(phases)], axis=0)
    return two_terms(forward), two_terms(forward.T / BLOCK)


def mxu(left, right):
    return jnp.dot(left, right, preferred_element_type=F32)


LANES = 128
VMEM = pl.BlockSpec(memory_space=pltpu.VMEM)
ANY = pl.BlockSpec(memory_space=pl.ANY)
MIB = 1024 * 1024


def cost(flops, size):
    return pl.CostEstimate(flops=int(flops), transcendentals=0, bytes_accessed=int(size))


def held(values):
    return pltpu.with_memory_space_constraint(values, pltpu.VMEM)


def streamed(values):
    return pltpu.with_memory_space_constraint(values, pltpu.HBM)


def whole(body, args, outs, scratch=(), limit=24, work=0, streams=(), out_streams=(), landed=()):
    size = sum(math.prod(a.shape) * a.dtype.itemsize for a in [*args, *outs])
    return pl.pallas_call(
        body,
        in_specs=[ANY if i in streams else VMEM for i in range(len(args))],
        out_specs=[ANY if i in out_streams else VMEM for i in range(len(outs))],
        out_shape=list(outs),
        scratch_shapes=list(scratch),
        cost_estimate=cost(work, size),
        compiler_params=pltpu.CompilerParams(vmem_limit_bytes=limit * MIB),
    )(*[streamed(a) if i in streams and i not in landed else a for i, a in enumerate(args)])


def kept(shape, dtype):
    return pltpu.VMEM(shape, dtype)


def stored(shape, dtype):
    return pltpu.HBM(shape, dtype)


def each(number, step):
    def body(index, carry):
        step(index)
        return carry

    lax.fori_loop(0, number, body, 0)


def copies(source, target, sems):
    return lambda j: pltpu.make_async_copy(source.at[j], target.at[j], sems.at[j])


def wide_copies(source, target, sems, width):
    lead = (slice(None),) * (len(source.shape) - 1)

    def move(j):
        here = pl.ds(pl.multiple_of(j * width, LANES), width)
        return pltpu.make_async_copy(source.at[(*lead, here)], target.at[j], sems.at[j])

    return move


def wide_stores(source, target, sems, width):
    lead = (slice(None),) * (len(target.shape) - 1)

    def move(j):
        here = pl.ds(pl.multiple_of(j * width, LANES), width)
        return pltpu.make_async_copy(source.at[j], target.at[(*lead, here)], sems.at[j])

    return move


def lane_tile(chunk, width, part=0, size=LANES):
    return pl.ds(pl.multiple_of(chunk * width + part * LANES, LANES), size)


def parts_of(width):
    return [(part, slice(part * LANES, (part + 1) * LANES)) for part in range(width // LANES)]


def to_chunks(values, width):
    tokens, local = values.shape
    count = local // width

    def body(source, target, rows, chunks, in_sems, out_sems):
        arrive = wide_copies(source, rows, in_sems, width)
        leave = copies(chunks, target, out_sems)
        for j in range(count):
            arrive(j).start()
        for j in range(count):
            arrive(j).wait()
            chunks[j] = rows[j].astype(BF16)
            leave(j).start()
        for j in range(count):
            leave(j).wait()

    return whole(
        body,
        [values],
        [stored((count, tokens, width), BF16)],
        [
            pltpu.VMEM((count, tokens, width), F32),
            pltpu.VMEM((count, tokens, width), BF16),
            pltpu.SemaphoreType.DMA((count,)),
            pltpu.SemaphoreType.DMA((count,)),
        ],
        streams=[0],
        out_streams=[0],
        limit=8,
    )[0]


def from_chunks(chunks):
    count, tokens, width = chunks.shape

    def body(source, target, rows, wide, in_sems, out_sems):
        arrive = copies(source, rows, in_sems)

        leave = wide_stores(wide, target, out_sems, width)
        for j in range(count):
            arrive(j).start()
        for j in range(count):
            arrive(j).wait()
            wide[j] = rows[j].astype(F32)
            leave(j).start()
        for j in range(count):
            leave(j).wait()

    return whole(
        body,
        [chunks],
        [stored((tokens, count * width), F32)],
        [
            pltpu.VMEM((count, tokens, width), BF16),
            pltpu.VMEM((count, tokens, width), F32),
            pltpu.SemaphoreType.DMA((count,)),
            pltpu.SemaphoreType.DMA((count,)),
        ],
        landed=[0],
        streams=[0],
        out_streams=[0],
        limit=8,
    )[0]


def three_terms(values):
    first = values.astype(BF16)
    rest = values - first.astype(F32)
    second = rest.astype(BF16)
    third = (rest - second.astype(F32)).astype(BF16)
    return first, second, third


def spread_taps(taps, local, width):
    rows, groups = taps.shape

    def body(t_ref, out_ref):
        terms = three_terms(t_ref[...])

        def step(j):
            group = lax.broadcasted_iota(jnp.int32, (groups, width), 0)
            channel = lax.broadcasted_iota(jnp.int32, (groups, width), 1)
            chosen = group == j * (width // GROUP) + channel // GROUP
            matrix = jnp.where(chosen, 1.0, 0.0).astype(BF16)
            total = mxu(terms[0], matrix) + (mxu(terms[1], matrix) + mxu(terms[2], matrix))
            out_ref[:, lane_tile(j, width, 0, width)] = total

        each(local // width, step)

    work = 4 * rows * groups * local
    return whole(body, [taps], [shape_of((rows, local), F32)], work=work)[0]


def gather_groups(sums, out_ref, groups, width):
    count, rows, _ = sums.shape
    per_chunk = width // GROUP
    group = lax.broadcasted_iota(jnp.int32, (width, LANES), 1)
    channel = lax.broadcasted_iota(jnp.int32, (width, LANES), 0)
    matrix = jnp.where(group == channel // GROUP, 1.0, 0.0).astype(BF16)
    terms = three_terms(sums[...].reshape(count * rows, width))
    found = mxu(terms[0], matrix) + (mxu(terms[1], matrix) + mxu(terms[2], matrix))
    for tile in range(groups // LANES):
        total = None
        for place in range(LANES // per_chunk):
            j = tile * (LANES // per_chunk) + place
            part = found[j * rows : (j + 1) * rows]
            part = pltpu.roll(part, place * per_chunk, axis=1) if place else part
            total = part if total is None else total + part
        out_ref[:, tile * LANES : (tile + 1) * LANES] = total


def dma(*shape):
    return pltpu.SemaphoreType.DMA(shape)


def short_conv(projections, edges, per_chan, width):
    _, tokens, local = projections.shape
    count = local // width

    def body(p_hbm, e_ref, t_ref, f_hbm, u_hbm, p_ref, feats, chunks, ext, p_sem, f_sem, u_sem):
        arrive = wide_copies(p_hbm, p_ref, p_sem, width)
        keep, leave = wide_stores(feats, f_hbm, f_sem, width), copies(chunks, u_hbm, u_sem)
        each(count, lambda j: arrive(j).start())

        def step(j):
            arrive(j).wait()
            for part, cols in parts_of(width):
                here = lane_tile(j, width, part)
                rows = t_ref[:, here]
                found = []
                for i in range(3):
                    ext[i, :HALO, :] = e_ref[i, :, here].astype(F32)
                    ext[i, HALO:, :] = p_ref[j, i, :, cols].astype(F32)
                    total = None
                    for tap in range(KS):
                        at = i * KS + tap
                        term = rows[at : at + 1] * ext[i, HALO - tap : HALO - tap + tokens, :]
                        total = term if total is None else total + term
                    found.append(total.astype(BF16))
                    feats[j, i, :, cols] = found[i]
                chunks[j, :, cols] = (found[1].astype(F32) * found[2].astype(F32)).astype(BF16)
            keep(j).start()
            leave(j).start()

        def finish(j):
            keep(j).wait()
            leave(j).wait()

        each(count, step)
        each(count, finish)

    return whole(
        body,
        [projections, edges, per_chan],
        [stored(projections.shape, BF16), stored((count, tokens, width), BF16)],
        [
            pltpu.VMEM((count, 3, tokens, width), BF16),
            pltpu.VMEM((count, 3, tokens, width), BF16),
            pltpu.VMEM((count, tokens, width), BF16),
            pltpu.VMEM((3, HALO + tokens, LANES), F32),
            dma(count),
            dma(count),
            dma(count),
        ],
        streams=[0],
        out_streams=[0, 1],
        work=42 * tokens * local,
    )


def window_spectrum(blocks, forward):
    count, _, width = blocks.shape
    half = BLOCK // 2

    def body(x_hbm, hi_hbm, lo_hbm, g_hbm, x_ref, hi, lo, g_ref, spec, t_sem, x_sem, g_sem):
        arrive, leave = copies(x_hbm, x_ref, x_sem), copies(g_ref, g_hbm, g_sem)
        moves = [
            pltpu.make_async_copy(hi_hbm, hi, t_sem.at[0]),
            pltpu.make_async_copy(lo_hbm, lo, t_sem.at[1]),
        ]
        for move in moves:
            move.start()
        for b in range(count):
            arrive(b).start()
        for move in moves:
            move.wait()
        for b in range(count):
            now, prev = b % 2, (b + 1) % 2
            arrive(b).wait()
            x = x_ref[b]
            spec[now] = mxu(hi[...], x) + mxu(lo[...], x)
            if b == 0:
                g_ref[0] = spec[0]
            else:
                g_ref[b, :half] = spec[now, :half] - spec[prev, BLOCK : BLOCK + half]
                g_ref[b, half:BLOCK] = spec[now, half:BLOCK] + spec[prev, BLOCK + half :]
                g_ref[b, BLOCK : BLOCK + half] = spec[now, BLOCK : BLOCK + half] + spec[prev, :half]
                g_ref[b, BLOCK + half :] = spec[now, BLOCK + half :] - spec[prev, half:BLOCK]
            leave(b).start()
        for b in range(count):
            leave(b).wait()

    shape = (count, 2 * BLOCK, width)
    return whole(
        body,
        [blocks, *forward],
        [stored(shape, F32)],
        [
            pltpu.VMEM(blocks.shape, BF16),
            *[pltpu.VMEM(table.shape, BF16) for table in forward],
            pltpu.VMEM(shape, F32),
            pltpu.VMEM((2, 2 * BLOCK, width), F32),
            dma(2),
            dma(count),
            dma(count),
        ],
        landed=[0],
        streams=[0, 1, 2],
        out_streams=[0],
        work=8 * BLOCK * blocks.size,
    )[0]


def block_products(window_ref, spec_ref, out_ref, count, width, adjoint):
    rows = 8

    def step(index):
        r = pl.multiple_of(index * rows, rows)
        for part, cols in parts_of(width):
            real = pl.ds(r, rows)
            imag = pl.ds(pl.multiple_of(r + BLOCK, rows), rows)
            win = [(window_ref[m, real, cols], window_ref[m, imag, cols]) for m in range(count)]
            spec = [(spec_ref[m, real, cols], spec_ref[m, imag, cols]) for m in range(count)]
            for b in range(count):
                acc_r = acc_i = None
                pairs = range(count - b) if adjoint else range(b + 1)
                for m in pairs:
                    wr, wi = win[m]
                    sr, si = spec[b + m] if adjoint else spec[b - m]
                    if adjoint:
                        tr, ti = wr * sr + wi * si, wr * si - wi * sr
                    else:
                        tr, ti = wr * sr - wi * si, wr * si + wi * sr
                    acc_r = tr if acc_r is None else acc_r + tr
                    acc_i = ti if acc_i is None else acc_i + ti
                out_ref[b, real, cols] = acc_r
                out_ref[b, imag, cols] = acc_i

    each(BLOCK // rows, step)


def inverse_block(prod, hi, lo):
    top = prod.astype(BF16)
    rest = (prod - top.astype(F32)).astype(BF16)
    return mxu(hi, top) + (mxu(lo, top) + mxu(hi, rest))


def convolve(blocks, window, tables, spread, adjoint):
    count, _, width = blocks.shape
    args = [blocks, window, *sum(tables, ())]

    def body(*refs):
        sources, refs = refs[:6], refs[6:]
        y_hbm, s_hbm, refs = (refs[0], refs[1], refs[2:]) if adjoint else (refs[0], None, refs[1:])
        x_ref, w_ref, fh, fl, th, tl, spec, prod, y_ref, t_sem, x_sem, y_sem, s_sem = refs
        arrive = copies(sources[0], x_ref, x_sem)
        shared, chunk, _ = y_hbm.shape
        tokens = count * BLOCK // shared

        def leave(i):
            rows = y_ref.at[i * tokens : i * tokens + chunk]
            return pltpu.make_async_copy(rows, y_hbm.at[i], y_sem.at[i])

        sent = 0
        loads = [
            pltpu.make_async_copy(sources[n], target, t_sem.at[n])
            for n, target in [(2, fh), (3, fl), (1, w_ref), (4, th), (5, tl)]
        ]
        loads[0].start()
        loads[1].start()
        for b in range(count):
            arrive(b).start()
        for move in loads[2:]:
            move.start()
        loads[0].wait()
        loads[1].wait()
        for b in range(count):
            arrive(b).wait()
            x = x_ref[b]
            spec[b] = mxu(fh[...], x) + mxu(fl[...], x)
            if adjoint:
                copies(spec, s_hbm, s_sem)(b).start()
        for move in loads[2:]:
            move.wait()
        block_products(w_ref, spec, prod, count, width, adjoint)
        y_ref[count * BLOCK :, :] = jnp.zeros((y_ref.shape[0] - count * BLOCK, width), BF16)
        for b in range(count):
            found = inverse_block(prod[b], th[...], tl[...])
            y_ref[b * BLOCK : (b + 1) * BLOCK, :] = found.astype(BF16)
            ready = y_ref.shape[0] if b == count - 1 else (b + 1) * BLOCK
            while sent < shared and sent * tokens + chunk <= ready:
                leave(sent).start()
                sent += 1
        for i in range(shared):
            leave(i).wait()
        if adjoint:
            for b in range(count):
                copies(spec, s_hbm, s_sem)(b).wait()

    extra = HALO if adjoint else 0
    tokens = count * BLOCK // spread
    outs = [stored((spread, tokens + extra, width), BF16)]
    if adjoint:
        outs.append(stored(window.shape, F32))
    return whole(
        body,
        args,
        outs,
        [
            *[pltpu.VMEM(a.shape, a.dtype) for a in args],
            pltpu.VMEM(window.shape, F32),
            pltpu.VMEM(window.shape, F32),
            pltpu.VMEM((count * BLOCK + 2 * HALO, width), BF16),
            dma(6),
            dma(count),
            dma(spread),
            dma(count),
        ],
        landed=[0],
        streams=range(6),
        out_streams=range(len(outs)),
        work=20 * BLOCK * blocks.size,
    )


def correlate(spectrum, window, inverse):
    count, _, width = spectrum.shape
    shape = (count, BLOCK, width)
    args = [spectrum, window, *inverse]

    def body(*refs):
        sources, y_hbm, targets = refs[:4], refs[4], refs[5:9]
        prod, y_ref, t_sem, y_sem = refs[9:]
        leave = copies(y_ref, y_hbm, y_sem)
        loads = [pltpu.make_async_copy(sources[n], targets[n], t_sem.at[n]) for n in range(4)]
        for move in loads:
            move.start()
        for move in loads:
            move.wait()
        s_ref, w_ref, th, tl = targets
        block_products(w_ref, s_ref, prod, count, width, True)
        for b in range(count):
            y_ref[b] = inverse_block(prod[b], th[...], tl[...]).astype(BF16)
            leave(b).start()
        for b in range(count):
            leave(b).wait()

    return whole(
        body,
        args,
        [stored(shape, BF16)],
        [
            *[pltpu.VMEM(a.shape, a.dtype) for a in args],
            pltpu.VMEM(window.shape, F32),
            pltpu.VMEM(shape, BF16),
            dma(4),
            dma(count),
        ],
        streams=range(4),
        out_streams=[0],
        work=12 * BLOCK * spectrum.size,
    )[0]


def row_sums(features, conv, gain, out_grad):
    count, tokens, width = conv.shape

    def body(q_hbm, c_hbm, g_ref, o_hbm, s_ref, q_ref, z_ref, o_ref, acc, q_sem, z_sem, o_sem):
        moves = [
            copies(c_hbm, z_ref, z_sem),
            wide_copies(q_hbm.at[0], q_ref, q_sem, width),
            wide_copies(o_hbm, o_ref, o_sem, width),
        ]

        def begin(j):
            for move in moves:
                move(j).start()

        each(count, begin)
        acc[...] = jnp.zeros_like(acc)

        def step(j):
            for move in moves:
                move(j).wait()
            for part, cols in parts_of(width):
                gated = q_ref[j, :, cols].astype(F32) * z_ref[j, :, cols].astype(F32)
                scaled = o_ref[j, :, cols].astype(F32) * g_ref[:, lane_tile(j, width, part)]
                acc[0] += gated * gated
                acc[1] += scaled * gated

        each(count, step)
        lane = lax.broadcasted_iota(jnp.int32, (tokens, LANES), 1)
        first = jnp.sum(acc[0], axis=1, keepdims=True)
        second = jnp.sum(acc[1], axis=1, keepdims=True)
        s_ref[...] = jnp.where(lane == 0, first, second).T[:8, :]

    return whole(
        body,
        [features, conv, gain, out_grad],
        [kept((8, tokens), F32), *[kept(conv.shape, BF16)] * 3],
        [pltpu.VMEM((2, tokens, LANES), F32), dma(count), dma(count), dma(count)],
        landed=[1],
        streams=[0, 1, 3],
        work=6 * conv.size,
    )


def row_scales(sums, tokens):
    turned = jnp.concatenate([sums] * (tokens // 8), axis=0).T
    rscale = lax.rsqrt(turned[:, 0:1] * (1.0 / D) + epsilon)
    return rscale, rscale * turned[:, 1:2] * (1.0 / D)


def conv_grads(gate, conv, out_grad, gain, own_sums, other_sums):
    count, tokens, width = conv.shape

    def body(q_ref, z_ref, o_ref, g_ref, s_ref, r_ref, d_hbm, t_hbm, chunks, total, d_sem, t_sem):
        leave = copies(chunks, d_hbm, d_sem)
        total[...] = s_ref[...] + r_ref[...]
        keep = pltpu.make_async_copy(total, t_hbm, t_sem.at[0])
        keep.start()
        rscale, inner = row_scales(total[...], tokens)
        factor = rscale * inner * rscale
        rscale = jnp.broadcast_to(rscale, (tokens, LANES))
        factor = jnp.broadcast_to(factor, (tokens, LANES))

        def step(j):
            for part, cols in parts_of(width):
                gate_feat = q_ref[j, :, cols].astype(F32)
                gated = gate_feat * z_ref[j, :, cols].astype(F32)
                scaled = o_ref[j, :, cols].astype(F32) * g_ref[:, lane_tile(j, width, part)]
                grad = (rscale * scaled - factor * gated) * gate_feat
                chunks[j, :, cols] = grad.astype(BF16)
            leave(j).start()

        each(count, step)
        keep.wait()
        each(count, lambda j: leave(j).wait())

    return whole(
        body,
        [*map(held, [gate, conv, out_grad]), gain, held(own_sums), other_sums],
        [stored(conv.shape, BF16), stored(own_sums.shape, F32)],
        [pltpu.VMEM(conv.shape, BF16), pltpu.VMEM(own_sums.shape, F32), dma(count), dma(1)],
        out_streams=[0, 1],
        work=8 * conv.size,
    )


def norm_outputs(features, conv, gain, out_grad, sums, projections, edges, groups):
    count, tokens, width = conv.shape
    local = count * width

    def body(q_hbm, c_hbm, g_ref, o_hbm, s_ref, p_hbm, e_ref, out_hbm, gg_hbm, rows_ref, *scratch):
        q_ref, z_ref, o_ref, p_ref, out, gg, ext, sums, gains, sems, out_sem, gg_sem = scratch
        moves = [
            copies(c_hbm, z_ref, sems.at[0]),
            wide_copies(q_hbm.at[0], q_ref, sems.at[1], width),
            wide_copies(o_hbm, o_ref, sems.at[2], width),
            wide_copies(p_hbm.at[0], p_ref, sems.at[3], width),
        ]
        stores = [wide_stores(out, out_hbm, out_sem, width), wide_stores(gg, gg_hbm, gg_sem, width)]

        def begin(j):
            for move in moves:
                move(j).start()

        each(count, begin)
        sums[...] = jnp.zeros_like(sums)
        rscale, inner = row_scales(s_ref[...], tokens)
        rscale = jnp.broadcast_to(rscale, (tokens, LANES))
        inner = jnp.broadcast_to(inner, (tokens, LANES))

        def step(j):
            for move in moves:
                move(j).wait()
            for part, cols in parts_of(width):
                here = lane_tile(j, width, part)
                conv_out = z_ref[j, :, cols].astype(F32)
                grad = o_ref[j, :, cols].astype(F32)
                gain_row = g_ref[:, here]
                normed = q_ref[j, :, cols].astype(F32) * conv_out * rscale
                out[j, :, cols] = (normed * gain_row).astype(BF16)
                grad_gated = rscale * (grad * gain_row - normed * inner)
                own = grad_gated * conv_out
                gg[j, :, cols] = own.astype(BF16)
                gains[:, here] = jnp.sum(grad * normed, axis=0, keepdims=True)
                before, values = e_ref[0, :, here], p_ref[j, :, cols]
                tap_sums(own, before, values, ext, sums, j, 0, cols, tokens)
            for store in stores:
                store(j).start()

        def finish(j):
            for store in stores:
                store(j).wait()

        each(count, step)
        for j in range(count):
            rows_ref[j : j + 1] = gains[:, j * width : (j + 1) * width]
        gather_groups(sums, rows_ref.at[count:], groups, width)
        each(count, finish)

    chunk = pltpu.VMEM(conv.shape, BF16)
    return whole(
        body,
        [features, conv, gain, out_grad, sums, projections, edges],
        [
            stored((tokens, local), BF16),
            stored((tokens, local), BF16),
            shape_of((count + KS + 1, groups), F32),
        ],
        [
            *[chunk] * 6,
            pltpu.VMEM((HALO + tokens, LANES), F32),
            pltpu.VMEM((count, KS + 1, width), F32),
            pltpu.VMEM((1, local), F32),
            dma(4, count),
            dma(count),
            dma(count),
        ],
        landed=[1],
        streams=[0, 1, 3, 5],
        out_streams=[0, 1],
        work=28 * conv.size,
    )


def shape_of(shape, dtype):
    return jax.ShapeDtypeStruct(shape, dtype)


def tap_sums(own, before, values, ext, sums, j, first, cols, tokens):
    ext[:HALO, :] = before.astype(F32)
    ext[HALO:, :] = values.astype(F32)
    for tap in range(KS):
        total = jnp.sum(own * ext[HALO - tap : HALO - tap + tokens, :], axis=0, keepdims=True)
        sums[j, first + tap : first + tap + 1, cols] = total


def mix_tap_sums(mix, features, projections, edges, groups):
    count, _, width = mix.shape
    tokens, local = features.shape[1:]

    def body(m_hbm, f_hbm, p_hbm, e_ref, out_ref, m_ref, f_ref, p_ref, ext, sums, sems):
        moves = [
            copies(m_hbm, m_ref, sems.at[0]),
            wide_copies(f_hbm.at[1:], f_ref, sems.at[1], width),
            wide_copies(p_hbm.at[1:], p_ref, sems.at[2], width),
        ]

        def begin(j):
            for move in moves:
                move(j).start()

        each(count, begin)
        sums[...] = jnp.zeros_like(sums)

        def step(j):
            for move in moves:
                move(j).wait()
            for part, cols in parts_of(width):
                here = lane_tile(j, width, part)
                mixed = m_ref[j, :tokens, cols].astype(F32)
                for i in (1, 2):
                    own = mixed * f_ref[j, 2 - i, :, cols].astype(F32)
                    before, values = e_ref[i, :, here], p_ref[j, i - 1, :, cols]
                    tap_sums(own, before, values, ext, sums, j, (i - 1) * KS, cols, tokens)

        each(count, step)
        gather_groups(sums, out_ref, groups, width)

    return whole(
        body,
        [mix, features, projections, edges],
        [shape_of((2 * KS + 2, groups), F32)],
        [
            pltpu.VMEM(mix.shape, BF16),
            pltpu.VMEM((count, 2, tokens, width), BF16),
            pltpu.VMEM((count, 2, tokens, width), BF16),
            pltpu.VMEM((HALO + tokens, LANES), F32),
            pltpu.VMEM((count, 2 * KS + 2, width), F32),
            dma(3, count),
        ],
        landed=[0],
        streams=[0, 1, 2],
        work=28 * tokens * local,
    )[0]


def proj_grads_of(mix, gate_grad, gate_halo, features, feat_halo, per_chan):
    count, _, width = mix.shape
    tokens, local = gate_grad.shape

    def body(m_hbm, gg_hbm, gh_ref, f_hbm, fh_ref, t_ref, o_hbm, *scratch):
        m_ref, gg_ref, f_ref, out, grads, sems, out_sem = scratch
        moves = [
            copies(m_hbm, m_ref, sems.at[0]),
            wide_copies(gg_hbm, gg_ref, sems.at[1], width),
            wide_copies(f_hbm.at[1:], f_ref, sems.at[2], width),
        ]
        leave = wide_stores(out, o_hbm, out_sem, width)

        def begin(j):
            for move in moves:
                move(j).start()

        each(count, begin)

        def step(j):
            for move in moves:
                move(j).wait()
            for part, cols in parts_of(width):
                here = lane_tile(j, width, part)
                rows = t_ref[:, here]
                mixed = m_ref[j, :tokens, cols].astype(F32)
                mixed_after = m_ref[j, tokens:, cols].astype(F32)
                for i in range(3):
                    if i == 0:
                        own = gg_ref[j, :, cols].astype(F32)
                        after = gh_ref[:, here].astype(F32)
                    else:
                        own = mixed * f_ref[j, 2 - i, :, cols].astype(F32)
                        after = mixed_after * fh_ref[3 - i, :, here].astype(F32)
                    grads[i, :tokens, :] = own
                    grads[i, tokens:, :] = after
                    total = None
                    for tap in range(KS):
                        at = i * KS + tap
                        term = rows[at : at + 1] * grads[i, tap : tap + tokens, :]
                        total = term if total is None else total + term
                    out[j, i, :, cols] = total.astype(BF16)
            leave(j).start()

        each(count, step)
        each(count, lambda j: leave(j).wait())

    return whole(
        body,
        [mix, gate_grad, gate_halo, features, feat_halo, per_chan],
        [stored((3, tokens, local), BF16)],
        [
            pltpu.VMEM(mix.shape, BF16),
            pltpu.VMEM((count, tokens, width), BF16),
            pltpu.VMEM((count, 2, tokens, width), BF16),
            pltpu.VMEM((count, 3, tokens, width), BF16),
            pltpu.VMEM((3, HALO + tokens, LANES), F32),
            dma(3, count),
            dma(count),
        ],
        landed=[0],
        streams=[0, 1, 3],
        out_streams=[0],
        work=48 * tokens * local,
    )[0]


def exchange(values, axis, distance):
    size = lax.axis_size(axis)
    return lax.ppermute(values, axis, [(i, i ^ distance) for i in range(size)])


def group_sum(values, axis, distances):
    first, second = distances
    others = [exchange(values, axis, d) for d in (first, second, first + second)]
    return (values + others[0]) + (others[1] + others[2])


def swap_blocks(chunks):
    return lax.all_to_all(chunks, "ctx", split_axis=0, concat_axis=0, tiled=True)


def together(*values):
    return lax.optimization_barrier(values)


def kernel_path(projections, grouped_short_filters, long_filter, norm_gain, out_grad):
    tokens, local = projections.shape[1:]
    spread = lax.axis_size("ctx")
    width = local // spread
    count = tokens * spread // BLOCK
    groups = local // GROUP

    def as_blocks(chunks):
        return chunks.reshape(count, BLOCK, width)

    def as_chunks(blocks):
        return blocks.reshape(spread, tokens, width)

    taps = jnp.pad(grouped_short_filters.reshape(3 * KS, groups), ((0, 3), (0, 0)))
    edges = passed_along(projections[:, tokens - HALO :, :], "ctx", 1)
    sent_h = to_chunks(long_filter, width)
    edges, sent_h = together(edges, sent_h)
    chan_h = swap_blocks(sent_h)
    tables = forward, inverse = jax.tree.map(jnp.asarray, block_tables())
    gain = norm_gain.reshape(1, local)
    per_chan = spread_taps(taps, local, width)
    features, mixed = short_conv(projections, edges, per_chan, width)
    chan_h, mixed = together(chan_h, mixed)
    chan_u = swap_blocks(mixed)
    window_h = window_spectrum(as_blocks(chan_h), forward)
    feat_halo = passed_along(features[:, :HALO, :], "ctx", -1)
    chan_u, window_h, feat_halo = together(chan_u, window_h, feat_halo)
    (chan_z,) = convolve(as_blocks(chan_u), window_h, tables, spread, False)
    conv = swap_blocks(chan_z)
    window_u = window_spectrum(as_blocks(chan_u), forward)
    conv, window_u = together(conv, window_u)
    own_sums, *near = row_sums(features, conv, gain, out_grad)
    grad_conv, sums = conv_grads(*near, gain, own_sums, exchange(own_sums, "ch", 1))
    chan_d = swap_blocks(grad_conv)
    output, gate_grad, early = norm_outputs(
        features, conv, gain, out_grad, sums, projections, edges, groups
    )
    gate_halo = passed_along(gate_grad[:HALO, :], "ctx", -1)
    early = group_sum(early, "ctx", (1, 2))
    early = early + exchange(early, "ctx", 4)
    chan_d, output, gate_grad, early = together(chan_d, output, gate_grad, early)
    chan_du, spec_d = convolve(as_blocks(chan_d), window_h, tables, spread, True)
    mix = swap_blocks(chan_du)
    early = early + exchange(early, "ctx", 8)
    chan_dh = correlate(spec_d, window_u, inverse)
    mix, chan_dh, gate_halo = together(mix, chan_dh, gate_halo)
    filt = swap_blocks(as_chunks(chan_dh))
    rows = mix_tap_sums(mix, features, projections, edges, groups)
    rows = group_sum(rows, "ctx", (1, 2))
    proj_grads = proj_grads_of(mix, gate_grad, gate_halo, features, feat_halo, per_chan)
    rows = group_sum(rows, "ctx", (4, 8))
    filt, proj_grads = together(filt, proj_grads)
    short_grads = jnp.stack([early[spread : spread + KS], rows[:KS], rows[KS : 2 * KS]])
    return (output, proj_grads, short_grads, from_chunks(filt), early[:spread].reshape(local))


def on_device(projections, grouped_short_filters, long_filter, norm_gain, out_grad):
    tokens, local = projections.shape[1:]
    spread = lax.axis_size("ctx")
    width = local // spread
    length = tokens * spread
    whole_tiles = width % LANES == 0 and tokens == LANES and length % BLOCK == 0
    pairs = spread == 16 and lax.axis_size("ch") == 2
    fits = whole_tiles and pairs and length <= 8 * BLOCK and width == local // GROUP
    path = kernel_path if fits else narrow_path
    return path(projections, grouped_short_filters, long_filter, norm_gain, out_grad)


def solution(mesh):
    in_specs = (P(None, "ctx", "ch"), P(None, None, "ch"), P("ctx", "ch"), P("ch"), P("ctx", "ch"))
    out_specs = (P("ctx", "ch"), P(None, "ctx", "ch"), P(None, None, "ch"), P("ctx", "ch"), P("ch"))
    return jax.shard_map(
        on_device, mesh=mesh, in_specs=in_specs, out_specs=out_specs, check_vma=False
    )
```
